128 devices in a mesh: rows: 32 (over y, z, core), feat: 4 (over x).
Axes of the slice: x: 4, y: 4, z: 4, core: 2. Of those that a mesh axis runs over, the one named last changes fastest.
Arguments:
- bin_codes: int32 [131072, 2048], P('rows', 'feat'), may hold values from 0 to 255
- gradient: bfloat16 [131072], P('rows'), may hold values from -6 to 6
- hessian: bfloat16 [131072], P('rows'), may hold values from 0.049804688 to 1
- leaf_of_block: int32 [1024], P('rows'), may hold values from 0 to 1
- block_rows: int32 [1024], P('rows'), may hold values from 32 to 128, as said below
Outputs:
- split_gain: float32 [2, 2048, 256], P(None, ('feat', 'rows'))
- best_gain: float32 [2], replicated
The draws below stay inside these ranges and needn't reach their ends.
Inputs may be any that keep to these rules, and one draw needn't show every extreme that they name: `block_rows`: the live rows are the first ones of their block; some block is full in every draw.
All inputs are finite; a program needn't handle non-finite values.
Results may differ from the reference program's by a relative error of at most 0.0003.
Values sent between devices are 32-bit elements; how exact they have to be, the bound alone decides.
A program may use at most 64 MiB of HBM per device.

```python
import math
import jax
import jax.numpy as jnp
import numpy as np
from jax import lax

FEATURES = 2048
BINS = 256
LEAVES = 2
BLOCK = 128
MIN_CHILD = 20
ROWS = 131072
BLOCKS = 1024


def draw_block_rows(key, part):
    first_key, second_key = jax.random.split(jax.random.fold_in(key, 17))
    live_rows = jax.random.randint(first_key, (BLOCKS,), BLOCK // 4, BLOCK + 1)
    full_block = jax.random.randint(second_key, (), 0, BLOCKS)
    return jnp.where(jnp.arange(BLOCKS) == full_block, BLOCK, live_rows).astype(jnp.int32)


def place_ends(values, rng, smallest, high):
    index_at = [jax.random.randint(jax.random.fold_in(rng, axis), (), 0, length) for axis, length in enumerate(values.shape)]
    main_axis = values.shape.index(max(values.shape))
    neighbour = index_at[:main_axis] + [(index_at[main_axis] + 1) % values.shape[main_axis]] + index_at[main_axis + 1:]
    return values.at[tuple(index_at)].set(smallest).at[tuple(neighbour)].set(high)


def level_of(stream_key, dims, pieces, least, high):
    gain, own = 1.0, jax.random.fold_in(stream_key, 6)
    for axis_at, parts in pieces:
        draws = jnp.exp(jax.random.uniform(jax.random.fold_in(own, axis_at), (parts,), jnp.float32, least / len(pieces), high / len(pieces)))
        gain = gain * jnp.repeat(draws, dims[axis_at] // parts).reshape([-1 if axis == axis_at else 1 for axis in range(len(dims))])
    return gain


def rank_table(number_of, slope):
    loads = [(1 << 20) // math.isqrt(rank ** slope) + 1 for rank in range(1, number_of + 1)]
    spread = 1 + sum(loads) // (1 << 30)
    return np.cumsum(np.array([max(1, weight // spread) for weight in loads]))


def ranked_ids(rng, dims, number_of, lean):
    table = rank_table(number_of, lean)
    pick = jax.random.randint(jax.random.fold_in(rng, 1), dims, 0, int(table[number_of - 1]))
    grade = jnp.searchsorted(jnp.asarray(table, jnp.int32), pick, side="right")
    return jax.random.permutation(jax.random.fold_in(rng, 2), number_of)[grade].astype(jnp.int32)


def centred(stream_key, extent, spread, most, shards=(), kind=jnp.bfloat16):
    values = spread * jax.random.normal(stream_key, extent, jnp.float32)
    if shards:
        values = values * level_of(stream_key, extent, shards, -0.22, 0.18)
    return jnp.clip(values, -most, most).astype(kind)


def setup_inputs(seed: int = 0) -> dict:
    splits = jax.random.split(jax.random.key(seed), 6)
    return {
        "bin_codes": place_ends(ranked_ids(splits[0], (ROWS, FEATURES), BINS, 2), jax.random.fold_in(splits[0], 3), 0, BINS - 1).astype(jnp.int32),
        "gradient": centred(splits[1], (ROWS,), 1.0, 6.0, ((0, 32),)),
        "hessian": jnp.clip(jnp.exp(math.log(1.0) - 2.9996462 * jax.random.uniform(splits[2], (ROWS,), jnp.float32) ** level_of(splits[2], (ROWS,), ((0, 32),), -0.2, 0.2)), 0.049804688, 1.0).astype(jnp.bfloat16),
        "leaf_of_block": place_ends(jax.random.randint(splits[3], (BLOCKS,), 0, LEAVES), jax.random.fold_in(splits[3], 1), 0, LEAVES - 1).astype(jnp.int32),
        "block_rows": draw_block_rows(jax.random.fold_in(splits[5], 71), 0),
    }


ridge_term = 1.0


def reference(bin_codes, gradient, hessian, leaf_of_block, block_rows):
    row_total = bin_codes.shape[0]
    feature_total = bin_codes.shape[1]
    offsets = jnp.arange(row_total, dtype=jnp.int32) % BLOCK
    live_rows = (offsets < jnp.repeat(block_rows, BLOCK)).astype(jnp.float32)
    leaf_ids = jnp.repeat(leaf_of_block, BLOCK).astype(jnp.int32)
    row_stats = jnp.stack([gradient.astype(jnp.float32), hessian.astype(jnp.float32), jnp.ones((row_total,), jnp.float32)], 1) * live_rows[:, None]

    def column_sums(column):
        return jax.ops.segment_sum(row_stats, leaf_ids * BINS + column, num_segments=LEAVES * BINS)

    histogram = lax.map(column_sums, bin_codes.T).reshape(feature_total, LEAVES, BINS, 3)
    running = jnp.cumsum(histogram, axis=2)
    totals = running[:, :, -1:, :]
    left_grad, left_hess, left_count = running[..., 0], running[..., 1], running[..., 2]
    total_grad, total_hess, total_count = totals[..., 0], totals[..., 1], totals[..., 2]
    right_grad = total_grad - left_grad
    right_hess = total_hess - left_hess
    right_count = total_count - left_count
    raw_gain = 0.5 * (left_grad ** 2 / (left_hess + ridge_term) + right_grad ** 2 / (right_hess + ridge_term) - total_grad ** 2 / (total_hess + ridge_term))
    allowed = (left_count >= MIN_CHILD) & (right_count >= MIN_CHILD)
    split_gain = jnp.transpose(jnp.where(allowed, raw_gain, 0.0), (1, 0, 2))
    best_gain = jnp.max(split_gain, axis=(1, 2))
    return split_gain, best_gain
```

```python
import functools
import jax
import jax.numpy as jnp
from jax import lax
from jax.experimental import pallas as pl
from jax.experimental.pallas import tpu as pltpu
from jax._src.pallas.mosaic.core import AccMemorySpace
from jax.sharding import PartitionSpec as P

BINS = 256
BLOCK = 128
LO = 32
HI = 8
FSTEP = 128
GROUP = 8


def hist_kernel(leaf_ref, live_ref, codes_ref, grad_ref, hess_ref, out_ref,
                compact, lo_ref, hi_ref, pair_ref, ones_ref, stat_ref, gf, hf):
    blocks = leaf_ref.shape[0]
    tiles = lo_ref.shape[0]
    first = pl.program_id(0) == 0

    def count(k, c):
        n = (live_ref[k] + 7) // 8 * 8
        one = leaf_ref[k]
        return c[0] + n * (1 - one), c[1] + n * one

    rows0, rows1 = lax.fori_loop(0, blocks, count, (jnp.int32(0), jnp.int32(0)))
    tiles0 = (rows0 + 255) // 256
    tiles1 = (rows1 + 255) // 256
    base1 = tiles0 * 256

    @pl.when(first)
    def _():
        gf[...] = grad_ref[...].astype(jnp.float32)
        hf[...] = hess_ref[...].astype(jnp.float32)
        stat_ref[...] = jnp.zeros_like(stat_ref)
        lane = lax.broadcasted_iota(jnp.int32, (8, 128), 1)
        sub = lax.broadcasted_iota(jnp.int32, (8, 128), 0)

        def place(k, off):
            n = live_ref[k]
            g = jnp.broadcast_to(gf[pl.ds(k, 1), :], (8, 128))
            h = jnp.broadcast_to(hf[pl.ds(k, 1), :], (8, 128))
            s = jnp.where(sub == 0, g, jnp.where(sub == 1, h, jnp.where(sub == 2, 1.0, 0.0)))
            s = jnp.where(lane < n, s, 0.0)
            shift = off % 128
            rolled = pltpu.roll(s, shift, 1)
            at = off // 128
            stat_ref[at] += jnp.where(lane >= shift, rolled, 0.0)
            stat_ref[at + 1] += jnp.where(lane < shift, rolled, 0.0)
            return off + (n + 7) // 8 * 8

        def pick(leaf, k, off):
            return lax.cond(leaf_ref[k] == leaf, lambda: place(k, off), lambda: off)

        lax.fori_loop(0, blocks, functools.partial(pick, 0), jnp.int32(0))
        lax.fori_loop(0, blocks, functools.partial(pick, 1), base1)

        @pl.loop(0, tiles)
        def _(t):
            for half in range(2):
                s = stat_ref[2 * t + half]
                g, h, c = (jnp.broadcast_to(s[i:i + 1, :], (8, 128)) for i in range(3))
                pair_ref[t, :, half * 128:half * 128 + 128] = jnp.concatenate([g, h], 0).astype(jnp.bfloat16)
                ones_ref[t, :, half * 128:half * 128 + 128] = jnp.concatenate([c, c], 0).astype(jnp.bfloat16)

    def move(leaf, k, off):
        def go():
            at = pl.multiple_of(off, 8)
            compact[pl.ds(at, BLOCK), :] = codes_ref[pl.ds(pl.multiple_of(k * BLOCK, BLOCK), BLOCK), :]
            return off + (live_ref[k] + 7) // 8 * 8
        return lax.cond(leaf_ref[k] == leaf, go, lambda: off)

    lax.fori_loop(0, blocks, functools.partial(move, 0), jnp.int32(0))
    lax.fori_loop(0, blocks, functools.partial(move, 1), base1)

    @pl.loop(0, (tiles0 + tiles1 + 1) // 2)
    def _(u):
        at = pl.multiple_of(u * 512, 512)
        word = compact[pl.ds(at, 128), :] & 255
        for q in range(1, 4):
            word = word | ((compact[pl.ds(at + 128 * q, 128), :] & 255) << (8 * q))
        word = word.T
        for q in range(4):
            lo = (word >> (8 * q)) & (LO - 1)
            hi = (word >> (8 * q + 5)) & (HI - 1)
            lanes = slice(128 * (q % 2), 128 * (q % 2) + 128)
            lo_ref[2 * u + q // 2, :, lanes] = lo.astype(jnp.float32)
            hi_ref[2 * u + q // 2, :, lanes] = hi.astype(jnp.float32)

    sub16 = lax.broadcasted_iota(jnp.int32, (16, 256), 0)
    lo_a = sub16.astype(jnp.float32).astype(jnp.bfloat16)
    lo_b = (sub16 + 16).astype(jnp.float32).astype(jnp.bfloat16)
    hi_n = (sub16 % 8).astype(jnp.float32).astype(jnp.bfloat16)
    one = jnp.ones((16, 256), jnp.bfloat16)
    zero = jnp.zeros((16, 256), jnp.bfloat16)
    lane_group = lax.broadcasted_iota(jnp.int32, (8, 128), 1) // LO

    groups = 8
    for leaf in range(2):
        for part in range(FSTEP // (groups * GROUP)):
            def run(*accs, leaf=leaf, part=part):
                def step(t, carry):
                    pair = pair_ref[t]
                    ones = ones_ref[t]
                    for i in range(groups):
                        rhs, lhs = [], []
                        for f2 in range(0, GROUP, 2):
                            his = []
                            for d in range(2):
                                f = part * groups * GROUP + i * GROUP + f2 + d
                                low = jnp.broadcast_to(lo_ref[t, f:f + 1, :], (16, 256)).astype(jnp.bfloat16)
                                rhs.append(jnp.where(low == lo_a, one, zero))
                                rhs.append(jnp.where(low == lo_b, one, zero))
                                high = jnp.broadcast_to(hi_ref[t, f:f + 1, :], (8, 256))
                                his.append(high)
                                high = jnp.concatenate([high, high], 0).astype(jnp.bfloat16)
                                lhs.append(jnp.where(high == hi_n, pair, zero))
                            both = jnp.concatenate(his, 0).astype(jnp.bfloat16)
                            lhs.append(jnp.where(both == hi_n, ones, zero))
                        stage = (i // 2) % 2
                        pltpu.matmul_push_rhs(jnp.concatenate(rhs, 0), stage, i % 2, transpose=True)
                        pltpu.matmul_acc_lhs(accs[i], jnp.concatenate(lhs, 0), load_staged_rhs=stage)
                    return carry

                lo_t = 0 if leaf == 0 else tiles0
                hi_t = tiles0 if leaf == 0 else tiles0 + tiles1
                lax.fori_loop(lo_t, hi_t, step, 0)
                for i in range(groups):
                    sums = pltpu.matmul_pop(accs[i])
                    for q in range(2):
                        for s in range(3):
                            tile = None
                            for d in range(4):
                                f = 4 * q + d
                                row = 48 * (f // 2) + (16 * (f % 2) + 8 * s if s < 2 else 32 + 8 * (f % 2))
                                piece = sums[row:row + 8, 128 * q:128 * q + 128]
                                tile = piece if tile is None else jnp.where(lane_group == d, piece, tile)
                            gq = (part * groups + i) * 2 + q
                            out_ref[gq // 4, leaf, gq % 4, s] = tile

            pl.run_scoped(run, *[AccMemorySpace(i % 2)((24 * GROUP, 256), jnp.float32) for i in range(groups)])


def local_hist(codes, grad, hess, leaf, live):
    rows, feats = codes.shape
    blocks = leaf.shape[0]
    tiles = rows // 256 + 2
    owners = FSTEP // 16
    spec = pltpu.PrefetchScalarGridSpec(
        num_scalar_prefetch=2,
        grid=(feats // FSTEP,),
        in_specs=[
            pl.BlockSpec((rows, FSTEP), lambda i, *_: (0, i)),
            pl.BlockSpec((blocks, BLOCK), lambda i, *_: (0, 0)),
            pl.BlockSpec((blocks, BLOCK), lambda i, *_: (0, 0)),
        ],
        out_specs=pl.BlockSpec((owners, 2, 4, 3, 8, 128), lambda i, *_: (i, 0, 0, 0, 0, 0)),
        scratch_shapes=[
            pltpu.VMEM((tiles * 256 + BLOCK, FSTEP), jnp.int32),
            pltpu.VMEM((tiles, FSTEP, 256), jnp.float32),
            pltpu.VMEM((tiles, FSTEP, 256), jnp.float32),
            pltpu.VMEM((tiles, 16, 256), jnp.bfloat16),
            pltpu.VMEM((tiles, 16, 256), jnp.bfloat16),
            pltpu.VMEM((2 * tiles + 1, 8, 128), jnp.float32),
            pltpu.VMEM((blocks, BLOCK), jnp.float32),
            pltpu.VMEM((blocks, BLOCK), jnp.float32),
        ],
    )
    return pl.pallas_call(
        hist_kernel,
        out_shape=jax.ShapeDtypeStruct((feats // 16, 2, 4, 3, 8, 128), jnp.float32),
        grid_spec=spec,
        name="histogram",
        compiler_params=pltpu.CompilerParams(vmem_limit_bytes=48 << 20),
    )(leaf, live, codes, grad.reshape(blocks, BLOCK), hess.reshape(blocks, BLOCK))


MIN_CHILD = 20
ridge_term = 1.0


def local(bin_codes, gradient, hessian, leaf_of_block, block_rows):
    mine = local_hist(bin_codes, gradient, hessian, leaf_of_block, block_rows)
    mine = lax.psum_scatter(mine, "rows", scatter_dimension=0, tiled=True)
    histogram = mine.reshape(2, 4, 3, HI, 4, LO).transpose(1, 4, 2, 0, 3, 5).reshape(16, 3, 2, BINS)
    running = jnp.cumsum(histogram, axis=3)
    totals = running[..., -1:]
    left_grad, left_hess, left_count = (running[:, 0], running[:, 1], running[:, 2])
    total_grad, total_hess, total_count = (totals[:, 0], totals[:, 1], totals[:, 2])
    right_grad = total_grad - left_grad
    right_hess = total_hess - left_hess
    right_count = total_count - left_count
    raw_gain = 0.5 * (
        left_grad**2 / (left_hess + ridge_term)
        + right_grad**2 / (right_hess + ridge_term)
        - total_grad**2 / (total_hess + ridge_term)
    )
    allowed = (left_count >= MIN_CHILD) & (right_count >= MIN_CHILD)
    split_gain = jnp.transpose(jnp.where(allowed, raw_gain, 0.0), (1, 0, 2))
    best_gain = lax.pmax(jnp.max(split_gain, axis=(1, 2)), ("rows", "feat"))
    return (split_gain, best_gain)


def solution(mesh):
    return jax.shard_map(
        local,
        mesh=mesh,
        in_specs=(P("rows", "feat"), P("rows"), P("rows"), P("rows"), P("rows")),
        out_specs=(P(None, ("feat", "rows"), None), P()),
        check_vma=False,
    )
```

```python
import functools
import jax
import jax.numpy as jnp
from jax import lax
from jax.experimental import pallas as pl
from jax.experimental.pallas import tpu as pltpu
from jax._src.pallas.mosaic.core import AccMemorySpace
from jax.sharding import PartitionSpec as P

BINS = 256
BLOCK = 128
LO = 32
HI = 8
FSTEP = 128
GROUP = 8


def hist_kernel(leaf_ref, live_ref, codes_ref, grad_ref, hess_ref, out_ref,
                compact, lo_ref, hi_ref, pair_ref, ones_ref, stat_ref, gf, hf):
    blocks = leaf_ref.shape[0]
    tiles = lo_ref.shape[0]
    first = pl.program_id(0) == 0

    def count(k, c):
        n = (live_ref[k] + 7) // 8 * 8
        one = leaf_ref[k]
        return c[0] + n * (1 - one), c[1] + n * one

    rows0, rows1 = lax.fori_loop(0, blocks, count, (jnp.int32(0), jnp.int32(0)))
    tiles0 = (rows0 + 255) // 256
    tiles1 = (rows1 + 255) // 256
    base1 = tiles0 * 256

    @pl.when(first)
    def _():
        gf[...] = grad_ref[...].astype(jnp.float32)
        hf[...] = hess_ref[...].astype(jnp.float32)
        stat_ref[...] = jnp.zeros_like(stat_ref)
        lane = lax.broadcasted_iota(jnp.int32, (8, 128), 1)
        sub = lax.broadcasted_iota(jnp.int32, (8, 128), 0)

        def place(k, off):
            n = live_ref[k]
            g = jnp.broadcast_to(gf[pl.ds(k, 1), :], (8, 128))
            h = jnp.broadcast_to(hf[pl.ds(k, 1), :], (8, 128))
            s = jnp.where(sub == 0, g, jnp.where(sub == 1, h, jnp.where(sub == 2, 1.0, 0.0)))
            s = jnp.where(lane < n, s, 0.0)
            shift = off % 128
            rolled = pltpu.roll(s, shift, 1)
            at = off // 128
            stat_ref[at] += jnp.where(lane >= shift, rolled, 0.0)
            stat_ref[at + 1] += jnp.where(lane < shift, rolled, 0.0)
            return off + (n + 7) // 8 * 8

        def pick(leaf, k, off):
            return lax.cond(leaf_ref[k] == leaf, lambda: place(k, off), lambda: off)

        lax.fori_loop(0, blocks, functools.partial(pick, 0), jnp.int32(0))
        lax.fori_loop(0, blocks, functools.partial(pick, 1), base1)

        @pl.loop(0, tiles)
        def _(t):
            for half in range(2):
                s = stat_ref[2 * t + half]
                g, h, c = (jnp.broadcast_to(s[i:i + 1, :], (8, 128)) for i in range(3))
                pair_ref[t, :, half * 128:half * 128 + 128] = jnp.concatenate([g, h], 0).astype(jnp.bfloat16)
                ones_ref[t, :, half * 128:half * 128 + 128] = jnp.concatenate([c, c], 0).astype(jnp.bfloat16)

    def move(leaf, k, off):
        def go():
            at = pl.multiple_of(off, 8)
            compact[pl.ds(at, BLOCK), :] = codes_ref[pl.ds(pl.multiple_of(k * BLOCK, BLOCK), BLOCK), :]
            return off + (live_ref[k] + 7) // 8 * 8
        return lax.cond(leaf_ref[k] == leaf, go, lambda: off)

    lax.fori_loop(0, blocks, functools.partial(move, 0), jnp.int32(0))
    lax.fori_loop(0, blocks, functools.partial(move, 1), base1)

    @pl.loop(0, (tiles0 + tiles1 + 1) // 2)
    def _(u):
        at = pl.multiple_of(u * 512, 512)
        word = compact[pl.ds(at, 128), :] & 255
        for q in range(1, 4):
            word = word | ((compact[pl.ds(at + 128 * q, 128), :] & 255) << (8 * q))
        word = word.T
        for q in range(4):
            lo = (word >> (8 * q)) & (LO - 1)
            hi = (word >> (8 * q + 5)) & (HI - 1)
            lanes = slice(128 * (q % 2), 128 * (q % 2) + 128)
            lo_ref[2 * u + q // 2, :, lanes] = lo.astype(jnp.float32)
            hi_ref[2 * u + q // 2, :, lanes] = hi.astype(jnp.float32)

    sub16 = lax.broadcasted_iota(jnp.int32, (16, 256), 0)
    lo_a = sub16.astype(jnp.float32).astype(jnp.bfloat16)
    lo_b = (sub16 + 16).astype(jnp.float32).astype(jnp.bfloat16)
    hi_n = (sub16 % 8).astype(jnp.float32).astype(jnp.bfloat16)
    one = jnp.ones((16, 256), jnp.bfloat16)
    zero = jnp.zeros((16, 256), jnp.bfloat16)
    lane_group = lax.broadcasted_iota(jnp.int32, (8, 128), 1) // LO

    groups = 8
    for leaf in range(2):
        for part in range(FSTEP // (groups * GROUP)):
            def run(*accs, leaf=leaf, part=part):
                def step(t, carry):
                    pair = pair_ref[t]
                    ones = ones_ref[t]
                    for i in range(groups):
                        rhs, lhs = [], []
                        for f2 in range(0, GROUP, 2):
                            his = []
                            for d in range(2):
                                f = part * groups * GROUP + i * GROUP + f2 + d
                                low = jnp.broadcast_to(lo_ref[t, f:f + 1, :], (16, 256)).astype(jnp.bfloat16)
                                rhs.append(jnp.where(low == lo_a, one, zero))
                                rhs.append(jnp.where(low == lo_b, one, zero))
                                high = jnp.broadcast_to(hi_ref[t, f:f + 1, :], (8, 256))
                                his.append(high)
                                high = jnp.concatenate([high, high], 0).astype(jnp.bfloat16)
                                lhs.append(jnp.where(high == hi_n, pair, zero))
                            both = jnp.concatenate(his, 0).astype(jnp.bfloat16)
                            lhs.append(jnp.where(both == hi_n, ones, zero))
                        stage = (i // 2) % 2
                        pltpu.matmul_push_rhs(jnp.concatenate(rhs, 0), stage, i % 2, transpose=True)
                        pltpu.matmul_acc_lhs(accs[i], jnp.concatenate(lhs, 0), load_staged_rhs=stage)
                    return carry

                lo_t = 0 if leaf == 0 else tiles0
                hi_t = tiles0 if leaf == 0 else tiles0 + tiles1
                lax.fori_loop(lo_t, hi_t, step, 0)
                for i in range(groups):
                    sums = pltpu.matmul_pop(accs[i])
                    for q in range(2):
                        for s in range(3):
                            tile = None
                            for d in range(4):
                                f = 4 * q + d
                                row = 48 * (f // 2) + (16 * (f % 2) + 8 * s if s < 2 else 32 + 8 * (f % 2))
                                piece = sums[row:row + 8, 128 * q:128 * q + 128]
                                tile = piece if tile is None else jnp.where(lane_group == d, piece, tile)
                            gq = (part * groups + i) * 2 + q
                            out_ref[gq // 4, leaf, gq % 4, s] = tile

            pl.run_scoped(run, *[AccMemorySpace(i % 2)((24 * GROUP, 256), jnp.float32) for i in range(groups)])


def local_hist(codes, grad, hess, leaf, live):
    rows, feats = codes.shape
    blocks = leaf.shape[0]
    tiles = rows // 256 + 2
    owners = FSTEP // 16
    spec = pltpu.PrefetchScalarGridSpec(
        num_scalar_prefetch=2,
        grid=(feats // FSTEP,),
        in_specs=[
            pl.BlockSpec((rows, FSTEP), lambda i, *_: (0, i)),
            pl.BlockSpec((blocks, BLOCK), lambda i, *_: (0, 0)),
            pl.BlockSpec((blocks, BLOCK), lambda i, *_: (0, 0)),
        ],
        out_specs=pl.BlockSpec((owners, 2, 4, 3, 8, 128), lambda i, *_: (i, 0, 0, 0, 0, 0)),
        scratch_shapes=[
            pltpu.VMEM((tiles * 256 + BLOCK, FSTEP), jnp.int32),
            pltpu.VMEM((tiles, FSTEP, 256), jnp.float32),
            pltpu.VMEM((tiles, FSTEP, 256), jnp.float32),
            pltpu.VMEM((tiles, 16, 256), jnp.bfloat16),
            pltpu.VMEM((tiles, 16, 256), jnp.bfloat16),
            pltpu.VMEM((2 * tiles + 1, 8, 128), jnp.float32),
            pltpu.VMEM((blocks, BLOCK), jnp.float32),
            pltpu.VMEM((blocks, BLOCK), jnp.float32),
        ],
    )
    return pl.pallas_call(
        hist_kernel,
        out_shape=jax.ShapeDtypeStruct((feats // 16, 2, 4, 3, 8, 128), jnp.float32),
        grid_spec=spec,
        name="histogram",
        compiler_params=pltpu.CompilerParams(vmem_limit_bytes=48 << 20),
    )(leaf, live, codes, grad.reshape(blocks, BLOCK), hess.reshape(blocks, BLOCK))


MESH = pl.DeviceIdType.MESH
MIN_CHILD = 20
ridge_term = 1.0


def finish(x):
    flat = x.reshape(192, 128)
    row = lax.broadcasted_iota(jnp.int32, (128, 256), 0)
    col = lax.broadcasted_iota(jnp.int32, (128, 256), 1)
    same = row // LO == (col % 128) // LO
    upper = jnp.where(same & ((row <= col) | (col >= 128)), 1.0, 0.0)
    sums = jnp.dot(flat, upper, precision=lax.Precision.HIGHEST, preferred_element_type=jnp.float32)
    sub = lax.broadcasted_iota(jnp.int32, (8, 128), 0)
    gains, tops = [], []
    for leaf in range(2):
        top = None
        for q in range(4):
            left, total = [], []
            for s in range(3):
                at = ((leaf * 4 + q) * 3 + s) * 8
                inner, whole = sums[at:at + 8, :128], sums[at:at + 8, 128:]
                run = whole
                for d in (1, 2, 4):
                    run = run + jnp.where(sub >= d, pltpu.roll(run, d, 0), 0.0)
                left.append(inner + (run - whole))
                total.append(jnp.broadcast_to(run[7:8, :], (8, 128)))
            right = [t - v for t, v in zip(total, left)]
            raw = 0.5 * (
                left[0] ** 2 / (left[1] + ridge_term)
                + right[0] ** 2 / (right[1] + ridge_term)
                - total[0] ** 2 / (total[1] + ridge_term)
            )
            allowed = (left[2] >= MIN_CHILD) & (right[2] >= MIN_CHILD)
            gain = jnp.where(allowed, raw, 0.0)
            gains.append(gain)
            top = gain if top is None else jnp.maximum(top, gain)
        tops.append(jnp.broadcast_to(jnp.max(top), (8, 128)))
    return gains, jnp.where(sub == 0, tops[0], tops[1])


def exchange_kernel(hist, gain_ref, best_ref, own, part, hop1, hop2, peak8, peak16,
                    load_sem, s0, r0, s1, r1, s2, r2, sa, ra, sb, rb):
    r = lax.axis_index("rows")
    x = lax.axis_index("feat")
    c = r % 2
    z = (r // 2) % 4
    y = r // 8
    at = (y, z)

    def rows_id(yy, zz, cc):
        return {"rows": (yy * 4 + zz) * 2 + cc, "feat": x}

    def along(axis, step):
        return rows_id((y + step) % 4, z, c) if axis == 0 else rows_id(y, (z + step) % 4, c)

    def octet(d):
        i = (x * 2 + c + d) % 8
        return {"rows": (y * 4 + z) * 2 + i % 2, "feat": i // 2}

    def plane(d):
        return {"rows": ((y * 4 + z + d) % 16) * 2 + c, "feat": x}

    barrier = pltpu.get_barrier_semaphore()
    for d in range(1, 8):
        pl.semaphore_signal(barrier, inc=1, device_id=octet(d), device_id_type=MESH)
    for d in range(1, 16):
        pl.semaphore_signal(barrier, inc=1, device_id=plane(d), device_id_type=MESH)

    order = (2, 1, 3, 0)

    def source(leaf, k, core):
        i = (at[leaf] + order[k]) % 4
        return hist.at[i, :, core, leaf] if leaf == 0 else hist.at[:, i, core, leaf]

    loads = [[pltpu.make_async_copy(source(leaf, k, c), own.at[leaf, k], load_sem.at[leaf, k])
              for k in range(4)] for leaf in range(2)]
    for k in range(4):
        for leaf in range(2):
            loads[leaf][k].start()
    pl.semaphore_wait(barrier, 22)

    pairs = [[pltpu.make_async_remote_copy(
        src_ref=source(leaf, k, 1 - c), dst_ref=part.at[leaf, k],
        send_sem=s0.at[leaf, k], recv_sem=r0.at[leaf, k],
        device_id=rows_id(y, z, 1 - c), device_id_type=MESH)
        for k in range(4)] for leaf in range(2)]
    for k in range(4):
        for leaf in range(2):
            pairs[leaf][k].start()

    def send1(leaf, way, i, k, b):
        return pltpu.make_async_remote_copy(
            src_ref=own.at[leaf, k, pl.ds(b, 2)], dst_ref=hop1.at[leaf, way, i],
            send_sem=s1.at[leaf, way, i], recv_sem=r1.at[leaf, way, i],
            device_id=along(leaf, 1 if way == 0 else 3), device_id_type=MESH)

    first = [[[send1(leaf, 0, 0, 0, 0), send1(leaf, 0, 1, 1, 2), send1(leaf, 0, 2, 1, 0)],
              [send1(leaf, 1, 0, 0, 2), send1(leaf, 1, 1, 2, 0), send1(leaf, 1, 2, 2, 2)]] for leaf in range(2)]

    def ready(leaf, k):
        loads[leaf][k].wait()
        pairs[leaf][k].wait_recv()
        own[leaf, k] = own[leaf, k] + part[leaf, k]

    for leaf in range(2):
        ready(leaf, 0)
        first[leaf][0][0].start()
        first[leaf][1][0].start()
    for leaf in range(2):
        ready(leaf, 1)
        first[leaf][0][1].start()
        ready(leaf, 2)
        first[leaf][1][1].start()
    for leaf in range(2):
        first[leaf][0][0].wait_recv()
        own[leaf, 1, 0:2] = own[leaf, 1, 0:2] + hop1[leaf, 0, 0]
        first[leaf][0][2].start()
        first[leaf][1][0].wait_recv()
        own[leaf, 2, 2:4] = own[leaf, 2, 2:4] + hop1[leaf, 1, 0]
        first[leaf][1][2].start()
    for leaf in range(2):
        ready(leaf, 3)

    def send2(leaf, way, i, step, row):
        b = (at[1 - leaf] + step) % 4
        return pltpu.make_async_remote_copy(
            src_ref=own.at[leaf, 3, b, pl.ds(row, 48)], dst_ref=hop2.at[leaf, way, i],
            send_sem=s2.at[leaf, way, i], recv_sem=r2.at[leaf, way, i],
            device_id=along(1 - leaf, 1 if way == 0 else 3), device_id_type=MESH)

    second = [[[send2(leaf, 0, 0, 2, 0), send2(leaf, 0, 1, 1, 48), send2(leaf, 0, 2, 1, 0)],
               [send2(leaf, 1, 0, 2, 48), send2(leaf, 1, 1, 3, 0), send2(leaf, 1, 2, 3, 48)]] for leaf in range(2)]
    for leaf in range(2):
        for way, i in ((0, 1), (1, 1), (0, 2), (1, 2)):
            first[leaf][way][i].wait_recv()
        own[leaf, 3, 0:2] = own[leaf, 3, 0:2] + (hop1[leaf, 0, 2] + hop1[leaf, 1, 1])
        own[leaf, 3, 2:4] = own[leaf, 3, 2:4] + (hop1[leaf, 0, 1] + hop1[leaf, 1, 2])
        second[leaf][0][0].start()
        second[leaf][1][0].start()
        second[leaf][0][1].start()
        second[leaf][1][1].start()
    for leaf in range(2):
        up, down = (at[1 - leaf] + 1) % 4, (at[1 - leaf] + 3) % 4
        second[leaf][0][0].wait_recv()
        own[leaf, 3, up, 0:48] = own[leaf, 3, up, 0:48] + hop2[leaf, 0, 0]
        second[leaf][0][2].start()
        second[leaf][1][0].wait_recv()
        own[leaf, 3, down, 48:96] = own[leaf, 3, down, 48:96] + hop2[leaf, 1, 0]
        second[leaf][1][2].start()
    mine = []
    for leaf in range(2):
        me = at[1 - leaf]
        for way, i in ((0, 1), (1, 1), (0, 2), (1, 2)):
            second[leaf][way][i].wait_recv()
        mine.append(own[leaf, 3, me, 0:48] + (hop2[leaf, 0, 2] + hop2[leaf, 1, 1]))
        mine.append(own[leaf, 3, me, 48:96] + (hop2[leaf, 0, 1] + hop2[leaf, 1, 2]))

    gains, top = finish(jnp.concatenate(mine, 0))
    for i, gain in enumerate(gains):
        gain_ref[i // 4, i % 4] = gain

    def spread(peaks, n, ssem, rsem, to):
        copies = [pltpu.make_async_remote_copy(
            src_ref=peaks.at[0], dst_ref=peaks.at[d], send_sem=ssem.at[d], recv_sem=rsem.at[d],
            device_id=to(d), device_id_type=MESH) for d in range(1, n)]
        for copy in copies:
            copy.start()
        for copy in copies:
            copy.wait()

    peak8[0] = top
    spread(peak8, 8, sa, ra, octet)
    peak16[0] = jnp.max(peak8[...], 0)
    spread(peak16, 16, sb, rb, plane)
    best_ref[...] = jnp.max(peak16[...], 0)

    for leaf in range(2):
        for k in range(4):
            pairs[leaf][k].wait_send()
        for way in range(2):
            for i in range(3):
                first[leaf][way][i].wait_send()
                second[leaf][way][i].wait_send()


def exchange(hist):
    dma = pltpu.SemaphoreType.DMA
    return pl.pallas_call(
        exchange_kernel,
        out_shape=(
            jax.ShapeDtypeStruct((2, 4, HI, 128), jnp.float32),
            jax.ShapeDtypeStruct((8, 128), jnp.float32),
        ),
        in_specs=[pl.BlockSpec(memory_space=pl.ANY)],
        out_specs=(pl.BlockSpec(memory_space=pltpu.VMEM), pl.BlockSpec(memory_space=pltpu.VMEM)),
        scratch_shapes=[
            pltpu.VMEM((2, 4, 4, 96, 128), jnp.float32),
            pltpu.VMEM((2, 4, 4, 96, 128), jnp.float32),
            pltpu.VMEM((2, 2, 3, 2, 96, 128), jnp.float32),
            pltpu.VMEM((2, 2, 3, 48, 128), jnp.float32),
            pltpu.VMEM((8, 8, 128), jnp.float32),
            pltpu.VMEM((16, 8, 128), jnp.float32),
            dma((2, 4)), dma((2, 4)), dma((2, 4)),
            dma((2, 2, 3)), dma((2, 2, 3)), dma((2, 2, 3)), dma((2, 2, 3)),
            dma((8,)), dma((8,)), dma((16,)), dma((16,)),
        ],
        name="exchange",
        compiler_params=pltpu.CompilerParams(collective_id=0, has_side_effects=True, vmem_limit_bytes=16 << 20),
    )(hist.reshape(4, 4, 2, 2, 96, 128))


def local(bin_codes, gradient, hessian, leaf_of_block, block_rows):
    mine = local_hist(bin_codes, gradient, hessian, leaf_of_block, block_rows)
    gain, best = exchange(mine)
    split_gain = gain.reshape(2, 4, HI, 4, LO).transpose(0, 1, 3, 2, 4).reshape(2, 16, BINS)
    return split_gain, best[:2, 0]


def solution(mesh):
    return jax.shard_map(
        local,
        mesh=mesh,
        in_specs=(P("rows", "feat"), P("rows"), P("rows"), P("rows"), P("rows")),
        out_specs=(P(None, ("feat", "rows"), None), P()),
        check_vma=False,
    )
```

```python
import jax
import jax.numpy as jnp
from jax import lax
from jax.experimental import pallas as pl
from jax.experimental.pallas import tpu as pltpu
from jax._src.pallas.mosaic.core import AccMemorySpace
from jax.sharding import PartitionSpec as P

BINS = 256
BLOCK = 128
LO = 32
HI = 8
FSTEP = 128
GROUP = 8
GROUPS = 8
TILE = 256


def hist_kernel(leaf_hbm, live_hbm, codes_hbm, grad_hbm, hess_hbm, out_hbm,
                leaf_ref, live_ref, table, codes_ref, grad_ref, hess_ref, lo_ref, hi_ref,
                g_ref, h_ref, c_ref, stat_ref, gf, hf, out_ref, small_sem, code_sem, out_sem):
    blocks = leaf_ref.shape[0]
    steps = codes_ref.shape[0]
    per_table = table.shape[0] // 2
    bf16 = jnp.bfloat16

    small = [pltpu.make_async_copy(a, b, small_sem.at[i]) for i, (a, b) in enumerate(
        ((leaf_hbm, leaf_ref), (live_hbm, live_ref), (grad_hbm, grad_ref), (hess_hbm, hess_ref)))]
    for copy in small:
        copy.start()

    def codes_copy(i):
        return pltpu.make_async_copy(
            codes_hbm.at[:, pl.ds(pl.multiple_of(i * FSTEP, FSTEP), FSTEP)], codes_ref.at[i], code_sem.at[i])

    codes_copy(0).start()
    stat_ref[...] = jnp.zeros_like(stat_ref)
    for copy in small:
        copy.wait()
    gf[...] = grad_ref[...].astype(jnp.float32)
    hf[...] = hess_ref[...].astype(jnp.float32)
    lane = lax.broadcasted_iota(jnp.int32, (8, 128), 1)
    sub = lax.broadcasted_iota(jnp.int32, (8, 128), 0)

    def place(k4, c):
        off0, off1 = c
        for d in range(4):
            k = k4 * 4 + d
            n = live_ref[k]
            leaf = leaf_ref[k]
            off = jnp.where(leaf == 0, off0, off1)
            for i in range(BLOCK // 8):
                table[leaf * per_table + off + i] = k * BLOCK + 8 * i
            g = jnp.broadcast_to(gf[pl.ds(k, 1), :], (8, 128))
            h = jnp.broadcast_to(hf[pl.ds(k, 1), :], (8, 128))
            s = jnp.where(sub == 0, g, jnp.where(sub == 1, h, jnp.where(sub == 2, 1.0, 0.0)))
            s = jnp.where(lane < n, s, 0.0)
            shift = off * 8 % 128
            rolled = pltpu.roll(s, shift, 1)
            at = off * 8 // 128
            stat_ref[leaf, at] += jnp.where(lane >= shift, rolled, 0.0)
            stat_ref[leaf, at + 1] += jnp.where(lane < shift, rolled, 0.0)
            off = off + (n + 7) // 8
            off0 = jnp.where(leaf == 0, off, off0)
            off1 = jnp.where(leaf == 0, off1, off)
        return off0, off1

    ends = lax.fori_loop(0, blocks // 4, place, (jnp.int32(0), jnp.int32(0)))
    tiles = [(end * 8 + TILE - 1) // TILE for end in ends]
    for leaf in range(2):
        for i in range(TILE // 8):
            table[leaf * per_table + ends[leaf] + i] = 0

        @pl.loop(0, tiles[leaf])
        def _(t):
            for half in range(2):
                s = stat_ref[leaf, 2 * t + half]
                for i, ref in enumerate((g_ref, h_ref, c_ref)):
                    ref[leaf, t, :, half * 128:half * 128 + 128] = jnp.broadcast_to(s[i:i + 1, :], (16, 128)).astype(bf16)

    sub8 = lax.broadcasted_iota(jnp.int32, (16, TILE), 0) % 8
    lo_n = [(sub8 + 8 * k).astype(jnp.float32).astype(bf16) for k in range(4)]
    hi_n = lo_n[0]
    one = jnp.ones((16, TILE), bf16)
    zero = jnp.zeros((16, TILE), bf16)
    which = 2 * (lane // 64) + lane // 8 % 2

    def turn(step, leaf, t, half):
        at = leaf * per_table + t * (TILE // 8) + half * (BLOCK // 8)
        rows = [codes_ref[step, pl.ds(pl.multiple_of(table[at + i], 8), 8), :] for i in range(BLOCK // 8)]
        word = jnp.concatenate(rows, 0).T
        lanes = slice(BLOCK * half, BLOCK * half + BLOCK)
        to = (0 if leaf == 0 else tiles[0]) + t
        lo_ref[step % 2, to, :, lanes] = (word & (LO - 1)).astype(jnp.float32)
        hi_ref[step % 2, to, :, lanes] = (word >> 5).astype(jnp.float32)

    codes_copy(0).wait()
    for i in range(1, steps):
        codes_copy(i).start()
    for leaf in range(2):
        @pl.loop(0, tiles[leaf])
        def _(t):
            for half in range(2):
                turn(0, leaf, t, half)

    @pl.loop(0, steps)
    def _(step):
        slot = step % 2
        later = jnp.minimum(step + 1, steps - 1)

        @pl.when(step + 1 < steps)
        def _():
            codes_copy(later).wait()

        for leaf in range(2):
            base = 0 if leaf == 0 else tiles[0]
            for half in range(FSTEP // (GROUPS * GROUP)):
                def run(*accs, leaf=leaf, half=half, base=base):
                    def pair(ref, t, i, p):
                        f = (half * GROUPS + i) * GROUP + 2 * p
                        return jnp.concatenate([jnp.broadcast_to(ref[slot, base + t, f + d:f + d + 1, :], (8, TILE))
                                                for d in range(2)], 0).astype(bf16)

                    def push(t, i):
                        rhs = []
                        for p in range(GROUP // 2):
                            low = pair(lo_ref, t, i, p)
                            rhs += [jnp.where(low == n, one, zero) for n in lo_n]
                        hot = jnp.concatenate(rhs, 0).astype(jnp.float8_e4m3fn)
                        pltpu.matmul_push_rhs(hot, (i // 2) % 2, i % 2, transpose=True)

                    def tile_step(t, carry):
                        stats = [ref[leaf, t] for ref in (g_ref, h_ref, c_ref)]
                        for i in range(GROUPS):
                            if i >= 2:
                                push(t, i)
                            lhs = []
                            for p in range(GROUP // 2):
                                hit = pair(hi_ref, t, i, p) == hi_n
                                lhs += [jnp.where(hit, s, zero) for s in stats]
                            pltpu.matmul_acc_lhs(accs[i], jnp.concatenate(lhs, 0), load_staged_rhs=(i // 2) % 2)
                        for i in range(2):
                            push(t + 1, i)
                        turn(later, leaf, t, half)
                        return carry

                    for i in range(2):
                        push(0, i)
                    lax.fori_loop(0, tiles[leaf], tile_step, 0)
                    for i in range(2):
                        pltpu.matmul_acc_lhs(accs[GROUPS + i], zero, load_staged_rhs=0)
                    for i in range(GROUPS):
                        sums = pltpu.matmul_pop(accs[i])
                        for q in range(2):
                            for s in range(3):
                                tile = None
                                for d in range(4):
                                    row = 48 * (2 * q + d // 2) + 16 * s + 8 * (d % 2)
                                    piece = sums[row:row + 8, 128 * q:128 * q + 128]
                                    tile = piece if tile is None else jnp.where(which == d, piece, tile)
                                gq = (half * GROUPS + i) * 2 + q
                                out_ref[step * (FSTEP // 16) + gq // 4, leaf, gq % 4, s] = tile

                pl.run_scoped(run, *[AccMemorySpace(i % 2)((24 * GROUP, 256), jnp.float32) for i in range(GROUPS)],
                              *[AccMemorySpace(i)((16, 256), jnp.float32) for i in range(2)])
        out_copy(out_ref, out_hbm, out_sem, step).start()

    for i in range(steps):
        out_copy(out_ref, out_hbm, out_sem, i).wait()


def out_copy(out_ref, out_hbm, out_sem, i):
    part = pl.ds(i * (FSTEP // 16), FSTEP // 16)
    return pltpu.make_async_copy(out_ref.at[part], out_hbm.at[part], out_sem.at[i])


def local_hist(codes, grad, hess, leaf, live):
    rows, feats = codes.shape
    blocks = leaf.shape[0]
    tiles = rows // TILE
    steps = feats // FSTEP
    hbm = pl.BlockSpec(memory_space=pltpu.HBM)
    out = (feats // 16, 2, 4, 3, 8, 128)
    dma = pltpu.SemaphoreType.DMA
    return pl.pallas_call(
        hist_kernel,
        out_shape=jax.ShapeDtypeStruct(out, jnp.float32),
        in_specs=[hbm] * 5,
        out_specs=hbm,
        scratch_shapes=[
            pltpu.SMEM((blocks,), jnp.int32),
            pltpu.SMEM((blocks,), jnp.int32),
            pltpu.SMEM((2 * (rows // 8 + TILE // 8 + 16),), jnp.int32),
            pltpu.VMEM((steps, rows, FSTEP), jnp.int32),
            pltpu.VMEM((blocks, BLOCK), jnp.bfloat16),
            pltpu.VMEM((blocks, BLOCK), jnp.bfloat16),
            pltpu.VMEM((2, tiles + 2, FSTEP, TILE), jnp.float32),
            pltpu.VMEM((2, tiles + 2, FSTEP, TILE), jnp.float32),
            pltpu.VMEM((2, tiles, 16, TILE), jnp.bfloat16),
            pltpu.VMEM((2, tiles, 16, TILE), jnp.bfloat16),
            pltpu.VMEM((2, tiles, 16, TILE), jnp.bfloat16),
            pltpu.VMEM((2, 2 * tiles + 2, 8, 128), jnp.float32),
            pltpu.VMEM((blocks, BLOCK), jnp.float32),
            pltpu.VMEM((blocks, BLOCK), jnp.float32),
            pltpu.VMEM(out, jnp.float32),
            dma((4,)), dma((steps,)), dma((steps,)),
        ],
        name="histogram",
        compiler_params=pltpu.CompilerParams(vmem_limit_bytes=67043328),
    )(leaf, live, codes, grad.reshape(blocks, BLOCK), hess.reshape(blocks, BLOCK))


MESH = pl.DeviceIdType.MESH
MIN_CHILD = 20
ridge_term = 1.0


def finish(x):
    flat = x.reshape(192, 128)
    row = lax.broadcasted_iota(jnp.int32, (128, 256), 0)
    col = lax.broadcasted_iota(jnp.int32, (128, 256), 1)
    same = 2 * (row // 64) + row // 8 % 2 == (col % 128) // LO
    upto = 8 * (row // 16 % 4) + row % 8 <= col % LO
    upper = jnp.where(same & (upto | (col >= 128)), 1.0, 0.0)
    sums = jnp.dot(flat, upper, precision=lax.Precision.HIGHEST, preferred_element_type=jnp.float32)
    sub = lax.broadcasted_iota(jnp.int32, (8, 128), 0)
    gains, tops = [], []
    for leaf in range(2):
        top = None
        for q in range(4):
            left, total = [], []
            for s in range(3):
                at = ((leaf * 4 + q) * 3 + s) * 8
                inner, whole = sums[at:at + 8, :128], sums[at:at + 8, 128:]
                run = whole
                for d in (1, 2, 4):
                    run = run + jnp.where(sub >= d, pltpu.roll(run, d, 0), 0.0)
                left.append(inner + (run - whole))
                total.append(jnp.broadcast_to(run[7:8, :], (8, 128)))
            right = [t - v for t, v in zip(total, left)]
            raw = 0.5 * (
                left[0] ** 2 / (left[1] + ridge_term)
                + right[0] ** 2 / (right[1] + ridge_term)
                - total[0] ** 2 / (total[1] + ridge_term)
            )
            allowed = (left[2] >= MIN_CHILD) & (right[2] >= MIN_CHILD)
            gain = jnp.where(allowed, raw, 0.0)
            gains.append(gain)
            top = gain if top is None else jnp.maximum(top, gain)
        tops.append(jnp.broadcast_to(jnp.max(top), (8, 128)))
    return gains, jnp.where(sub == 0, tops[0], tops[1])


def exchange_kernel(hist, gain_ref, best_ref, own, part, hop1, hop2, peak8, peak16,
                    load_sem, s0, r0, s1, r1, s2, r2, sa, ra, sb, rb):
    r = lax.axis_index("rows")
    x = lax.axis_index("feat")
    c = r % 2
    z = (r // 2) % 4
    y = r // 8
    at = (y, z)

    def rows_id(yy, zz, cc):
        return {"rows": (yy * 4 + zz) * 2 + cc, "feat": x}

    def along(axis, step):
        return rows_id((y + step) % 4, z, c) if axis == 0 else rows_id(y, (z + step) % 4, c)

    def octet(d):
        i = (x * 2 + c + d) % 8
        return {"rows": (y * 4 + z) * 2 + i % 2, "feat": i // 2}

    def plane(d):
        return {"rows": ((y * 4 + z + d) % 16) * 2 + c, "feat": x}

    barrier = pltpu.get_barrier_semaphore()
    for d in range(1, 8):
        pl.semaphore_signal(barrier, inc=1, device_id=octet(d), device_id_type=MESH)
    for d in range(1, 16):
        pl.semaphore_signal(barrier, inc=1, device_id=plane(d), device_id_type=MESH)

    order = (2, 1, 3, 0)

    def source(leaf, k, core):
        i = (at[leaf] + order[k]) % 4
        return hist.at[i, :, core, leaf] if leaf == 0 else hist.at[:, i, core, leaf]

    loads = [[pltpu.make_async_copy(source(leaf, k, c), own.at[leaf, k], load_sem.at[leaf, k])
              for k in range(4)] for leaf in range(2)]
    for k in range(4):
        for leaf in range(2):
            loads[leaf][k].start()
    pl.semaphore_wait(barrier, 22)

    pairs = [[pltpu.make_async_remote_copy(
        src_ref=source(leaf, k, 1 - c), dst_ref=part.at[leaf, k],
        send_sem=s0.at[leaf, k], recv_sem=r0.at[leaf, k],
        device_id=rows_id(y, z, 1 - c), device_id_type=MESH)
        for k in range(4)] for leaf in range(2)]
    for k in range(4):
        for leaf in range(2):
            pairs[leaf][k].start()

    def send1(leaf, way, i, k, b):
        return pltpu.make_async_remote_copy(
            src_ref=own.at[leaf, k, pl.ds(b, 2)], dst_ref=hop1.at[leaf, way, i],
            send_sem=s1.at[leaf, way, i], recv_sem=r1.at[leaf, way, i],
            device_id=along(leaf, 1 if way == 0 else 3), device_id_type=MESH)

    first = [[[send1(leaf, 0, 0, 0, 0), send1(leaf, 0, 1, 1, 2), send1(leaf, 0, 2, 1, 0)],
              [send1(leaf, 1, 0, 0, 2), send1(leaf, 1, 1, 2, 0), send1(leaf, 1, 2, 2, 2)]] for leaf in range(2)]

    def ready(leaf, k):
        loads[leaf][k].wait()
        pairs[leaf][k].wait_recv()
        own[leaf, k] = own[leaf, k] + part[leaf, k]

    for leaf in range(2):
        ready(leaf, 0)
        first[leaf][0][0].start()
        first[leaf][1][0].start()
    for leaf in range(2):
        ready(leaf, 1)
        first[leaf][0][1].start()
        ready(leaf, 2)
        first[leaf][1][1].start()
    for leaf in range(2):
        first[leaf][0][0].wait_recv()
        own[leaf, 1, 0:2] = own[leaf, 1, 0:2] + hop1[leaf, 0, 0]
        first[leaf][0][2].start()
        first[leaf][1][0].wait_recv()
        own[leaf, 2, 2:4] = own[leaf, 2, 2:4] + hop1[leaf, 1, 0]
        first[leaf][1][2].start()
    for leaf in range(2):
        ready(leaf, 3)

    def send2(leaf, way, i, step, row):
        b = (at[1 - leaf] + step) % 4
        return pltpu.make_async_remote_copy(
            src_ref=own.at[leaf, 3, b, pl.ds(row, 48)], dst_ref=hop2.at[leaf, way, i],
            send_sem=s2.at[leaf, way, i], recv_sem=r2.at[leaf, way, i],
            device_id=along(1 - leaf, 1 if way == 0 else 3), device_id_type=MESH)

    second = [[[send2(leaf, 0, 0, 2, 0), send2(leaf, 0, 1, 1, 48), send2(leaf, 0, 2, 1, 0)],
               [send2(leaf, 1, 0, 2, 48), send2(leaf, 1, 1, 3, 0), send2(leaf, 1, 2, 3, 48)]] for leaf in range(2)]
    for leaf in range(2):
        for way, i in ((0, 1), (1, 1), (0, 2), (1, 2)):
            first[leaf][way][i].wait_recv()
        own[leaf, 3, 0:2] = own[leaf, 3, 0:2] + (hop1[leaf, 0, 2] + hop1[leaf, 1, 1])
        own[leaf, 3, 2:4] = own[leaf, 3, 2:4] + (hop1[leaf, 0, 1] + hop1[leaf, 1, 2])
        second[leaf][0][0].start()
        second[leaf][1][0].start()
        second[leaf][0][1].start()
        second[leaf][1][1].start()
    for leaf in range(2):
        up, down = (at[1 - leaf] + 1) % 4, (at[1 - leaf] + 3) % 4
        second[leaf][0][0].wait_recv()
        own[leaf, 3, up, 0:48] = own[leaf, 3, up, 0:48] + hop2[leaf, 0, 0]
        second[leaf][0][2].start()
        second[leaf][1][0].wait_recv()
        own[leaf, 3, down, 48:96] = own[leaf, 3, down, 48:96] + hop2[leaf, 1, 0]
        second[leaf][1][2].start()
    mine = []
    for leaf in range(2):
        me = at[1 - leaf]
        for way, i in ((0, 1), (1, 1), (0, 2), (1, 2)):
            second[leaf][way][i].wait_recv()
        mine.append(own[leaf, 3, me, 0:48] + (hop2[leaf, 0, 2] + hop2[leaf, 1, 1]))
        mine.append(own[leaf, 3, me, 48:96] + (hop2[leaf, 0, 1] + hop2[leaf, 1, 2]))

    gains, top = finish(jnp.concatenate(mine, 0))
    for i, gain in enumerate(gains):
        gain_ref[i // 4, i % 4] = gain

    def spread(peaks, n, ssem, rsem, to):
        copies = [pltpu.make_async_remote_copy(
            src_ref=peaks.at[0], dst_ref=peaks.at[d], send_sem=ssem.at[d], recv_sem=rsem.at[d],
            device_id=to(d), device_id_type=MESH) for d in range(1, n)]
        for copy in copies:
            copy.start()
        for copy in copies:
            copy.wait()

    peak8[0] = top
    spread(peak8, 8, sa, ra, octet)
    peak16[0] = jnp.max(peak8[...], 0)
    spread(peak16, 16, sb, rb, plane)
    best_ref[...] = jnp.max(peak16[...], 0)

    for leaf in range(2):
        for k in range(4):
            pairs[leaf][k].wait_send()
        for way in range(2):
            for i in range(3):
                first[leaf][way][i].wait_send()
                second[leaf][way][i].wait_send()


def exchange(hist):
    dma = pltpu.SemaphoreType.DMA
    return pl.pallas_call(
        exchange_kernel,
        out_shape=(
            jax.ShapeDtypeStruct((2, 4, HI, 128), jnp.float32),
            jax.ShapeDtypeStruct((8, 128), jnp.float32),
        ),
        in_specs=[pl.BlockSpec(memory_space=pl.ANY)],
        out_specs=(pl.BlockSpec(memory_space=pltpu.VMEM), pl.BlockSpec(memory_space=pltpu.VMEM)),
        scratch_shapes=[
            pltpu.VMEM((2, 4, 4, 96, 128), jnp.float32),
            pltpu.VMEM((2, 4, 4, 96, 128), jnp.float32),
            pltpu.VMEM((2, 2, 3, 2, 96, 128), jnp.float32),
            pltpu.VMEM((2, 2, 3, 48, 128), jnp.float32),
            pltpu.VMEM((8, 8, 128), jnp.float32),
            pltpu.VMEM((16, 8, 128), jnp.float32),
            dma((2, 4)), dma((2, 4)), dma((2, 4)),
            dma((2, 2, 3)), dma((2, 2, 3)), dma((2, 2, 3)), dma((2, 2, 3)),
            dma((8,)), dma((8,)), dma((16,)), dma((16,)),
        ],
        name="exchange",
        compiler_params=pltpu.CompilerParams(collective_id=0, has_side_effects=True, vmem_limit_bytes=67043328),
    )(hist.reshape(4, 4, 2, 2, 96, 128))


def local(bin_codes, gradient, hessian, leaf_of_block, block_rows):
    mine = local_hist(bin_codes, gradient, hessian, leaf_of_block, block_rows)
    gain, best = exchange(mine)
    split_gain = gain.reshape(2, 4, HI, 4, LO).transpose(0, 1, 3, 2, 4).reshape(2, 16, BINS)
    return split_gain, best[:2, 0]


def solution(mesh):
    return jax.shard_map(
        local,
        mesh=mesh,
        in_specs=(P("rows", "feat"), P("rows"), P("rows"), P("rows"), P("rows")),
        out_specs=(P(None, ("feat", "rows"), None), P()),
        check_vma=False,
    )
```

```python
import jax
import jax.numpy as jnp
from jax import lax
from jax.experimental import pallas as pl
from jax.experimental.pallas import tpu as pltpu
from jax._src.pallas.mosaic.core import AccMemorySpace
from jax.sharding import PartitionSpec as P

BINS = 256
BLOCK = 128
LO = 32
HI = 8
FSTEP = 128
GROUP = 8
GROUPS = 8
TILE = 256


def hist_kernel(leaf_hbm, live_hbm, codes_hbm, grad_hbm, hess_hbm, out_hbm,
                leaf_ref, live_ref, table, codes_ref, grad_ref, hess_ref, lo_ref, hi_ref,
                g_ref, h_ref, c_ref, stat_ref, gf, hf, out_ref, small_sem, code_sem, out_sem):
    blocks = leaf_ref.shape[0]
    steps = codes_ref.shape[0]
    per_table = table.shape[0] // 2
    bf16 = jnp.bfloat16

    small = [pltpu.make_async_copy(a, b, small_sem.at[i]) for i, (a, b) in enumerate(
        ((leaf_hbm, leaf_ref), (live_hbm, live_ref), (grad_hbm, grad_ref), (hess_hbm, hess_ref)))]
    for copy in small:
        copy.start()

    def codes_copy(i):
        return pltpu.make_async_copy(
            codes_hbm.at[:, pl.ds(pl.multiple_of(i * FSTEP, FSTEP), FSTEP)], codes_ref.at[i], code_sem.at[i])

    codes_copy(0).start()
    stat_ref[...] = jnp.zeros_like(stat_ref)
    for copy in small:
        copy.wait()
    gf[...] = grad_ref[...].astype(jnp.float32)
    hf[...] = hess_ref[...].astype(jnp.float32)
    lane = lax.broadcasted_iota(jnp.int32, (8, 128), 1)
    sub = lax.broadcasted_iota(jnp.int32, (8, 128), 0)

    def place(k4, c):
        off0, off1 = c
        for d in range(4):
            k = k4 * 4 + d
            n = live_ref[k]
            leaf = leaf_ref[k]
            off = jnp.where(leaf == 0, off0, off1)
            to = leaf * per_table + off
            shift = k * BLOCK - 8 * off
            for i in range(BLOCK // 8):
                table[to + i] = shift
            g = jnp.broadcast_to(gf[pl.ds(k, 1), :], (8, 128))
            h = jnp.broadcast_to(hf[pl.ds(k, 1), :], (8, 128))
            s = jnp.where(sub == 0, g, jnp.where(sub == 1, h, jnp.where(sub == 2, 1.0, 0.0)))
            s = jnp.where(lane < n, s, 0.0)
            turned = lax.rem(off, 16) * 8
            rolled = pltpu.roll(s, turned, 1)
            at = off // 16
            stat_ref[leaf, at] += jnp.where(lane >= turned, rolled, 0.0)
            stat_ref[leaf, at + 1] += jnp.where(lane < turned, rolled, 0.0)
            off = off + (n + 7) // 8
            off0 = jnp.where(leaf == 0, off, off0)
            off1 = jnp.where(leaf == 0, off1, off)
        return off0, off1

    ends = lax.fori_loop(0, blocks // 4, place, (jnp.int32(0), jnp.int32(0)))
    tiles = [(end * 8 + TILE - 1) // TILE for end in ends]
    for leaf in range(2):
        for i in range(TILE // 8):
            table[leaf * per_table + ends[leaf] + i] = -8 * ends[leaf]

        @pl.loop(0, tiles[leaf])
        def _(t):
            for half in range(2):
                s = stat_ref[leaf, 2 * t + half]
                for i, ref in enumerate((g_ref, h_ref, c_ref)):
                    ref[leaf, t, :, half * 128:half * 128 + 128] = jnp.broadcast_to(s[i:i + 1, :], (16, 128)).astype(bf16)

    sub8 = lax.broadcasted_iota(jnp.int32, (16, TILE), 0) % 8
    lo_n = [(sub8 + 8 * k).astype(jnp.float32).astype(bf16) for k in range(4)]
    hi_n = lo_n[0]
    one = jnp.ones((16, TILE), bf16)
    zero = jnp.zeros((16, TILE), bf16)
    which = 2 * (lane // 64) + lane // 8 % 2

    def turn(step, leaf, t, half):
        first = t * (TILE // 8) + half * (BLOCK // 8)
        rows = [codes_ref[step, pl.ds(pl.multiple_of(table[leaf * per_table + first + i] + 8 * (first + i), 8), 8), :]
                for i in range(BLOCK // 8)]
        word = jnp.concatenate(rows, 0).T
        lanes = slice(BLOCK * half, BLOCK * half + BLOCK)
        to = (0 if leaf == 0 else tiles[0]) + t
        lo_ref[step % 2, to, :, lanes] = (word & (LO - 1)).astype(jnp.float32)
        hi_ref[step % 2, to, :, lanes] = (word >> 5).astype(jnp.float32)

    codes_copy(0).wait()
    for i in range(1, steps):
        codes_copy(i).start()
    for leaf in range(2):
        @pl.loop(0, tiles[leaf])
        def _(t):
            for half in range(2):
                turn(0, leaf, t, half)

    @pl.loop(0, steps)
    def _(step):
        slot = step % 2
        later = jnp.minimum(step + 1, steps - 1)

        @pl.when(step + 1 < steps)
        def _():
            codes_copy(later).wait()

        for leaf in range(2):
            base = 0 if leaf == 0 else tiles[0]
            for half in range(FSTEP // (GROUPS * GROUP)):
                def run(*accs, leaf=leaf, half=half, base=base):
                    def pair(ref, t, i, p):
                        f = (half * GROUPS + i) * GROUP + 2 * p
                        return jnp.concatenate([jnp.broadcast_to(ref[slot, base + t, f + d:f + d + 1, :], (8, TILE))
                                                for d in range(2)], 0).astype(bf16)

                    def push(t, i):
                        rhs = []
                        for p in range(GROUP // 2):
                            low = pair(lo_ref, t, i, p)
                            rhs += [jnp.where(low == n, one, zero) for n in lo_n]
                        hot = jnp.concatenate(rhs, 0).astype(jnp.float8_e4m3fn)
                        pltpu.matmul_push_rhs(hot, (i // 2) % 2, i % 2, transpose=True)

                    def tile_step(t, carry):
                        stats = [ref[leaf, t] for ref in (g_ref, h_ref, c_ref)]
                        for i in range(GROUPS):
                            if i >= 2:
                                push(t, i)
                            lhs = []
                            for p in range(GROUP // 2):
                                hit = pair(hi_ref, t, i, p) == hi_n
                                lhs += [jnp.where(hit, s, zero) for s in stats]
                            pltpu.matmul_acc_lhs(accs[i], jnp.concatenate(lhs, 0), load_staged_rhs=(i // 2) % 2)
                        for i in range(2):
                            push(t + 1, i)
                        turn(later, leaf, t, half)
                        return carry

                    for i in range(2):
                        push(0, i)
                    lax.fori_loop(0, tiles[leaf], tile_step, 0)
                    for i in range(2):
                        pltpu.matmul_acc_lhs(accs[GROUPS + i], zero, load_staged_rhs=0)
                    for i in range(GROUPS):
                        sums = pltpu.matmul_pop(accs[i])
                        for q in range(2):
                            for s in range(3):
                                tile = None
                                for d in range(4):
                                    row = 48 * (2 * q + d // 2) + 16 * s + 8 * (d % 2)
                                    piece = sums[row:row + 8, 128 * q:128 * q + 128]
                                    tile = piece if tile is None else jnp.where(which == d, piece, tile)
                                gq = (half * GROUPS + i) * 2 + q
                                out_ref[step * (FSTEP // 16) + gq // 4, leaf, gq % 4, s] = tile

                pl.run_scoped(run, *[AccMemorySpace(i % 2)((24 * GROUP, 256), jnp.float32) for i in range(GROUPS)],
                              *[AccMemorySpace(i)((16, 256), jnp.float32) for i in range(2)])
        out_copy(out_ref, out_hbm, out_sem, step).start()

    for i in range(steps):
        out_copy(out_ref, out_hbm, out_sem, i).wait()


def out_copy(out_ref, out_hbm, out_sem, i):
    part = pl.ds(i * (FSTEP // 16), FSTEP // 16)
    return pltpu.make_async_copy(out_ref.at[part], out_hbm.at[part], out_sem.at[i])


def local_hist(codes, grad, hess, leaf, live):
    rows, feats = codes.shape
    blocks = leaf.shape[0]
    tiles = rows // TILE
    steps = feats // FSTEP
    hbm = pl.BlockSpec(memory_space=pltpu.HBM)
    out = (feats // 16, 2, 4, 3, 8, 128)
    dma = pltpu.SemaphoreType.DMA
    return pl.pallas_call(
        hist_kernel,
        out_shape=jax.ShapeDtypeStruct(out, jnp.float32),
        in_specs=[hbm] * 5,
        out_specs=hbm,
        scratch_shapes=[
            pltpu.SMEM((blocks,), jnp.int32),
            pltpu.SMEM((blocks,), jnp.int32),
            pltpu.SMEM((2 * (rows // 8 + TILE // 8 + 16),), jnp.int32),
            pltpu.VMEM((steps, rows, FSTEP), jnp.int32),
            pltpu.VMEM((blocks, BLOCK), jnp.bfloat16),
            pltpu.VMEM((blocks, BLOCK), jnp.bfloat16),
            pltpu.VMEM((2, tiles + 2, FSTEP, TILE), jnp.float32),
            pltpu.VMEM((2, tiles + 2, FSTEP, TILE), jnp.float32),
            pltpu.VMEM((2, tiles, 16, TILE), jnp.bfloat16),
            pltpu.VMEM((2, tiles, 16, TILE), jnp.bfloat16),
            pltpu.VMEM((2, tiles, 16, TILE), jnp.bfloat16),
            pltpu.VMEM((2, 2 * tiles + 2, 8, 128), jnp.float32),
            pltpu.VMEM((blocks, BLOCK), jnp.float32),
            pltpu.VMEM((blocks, BLOCK), jnp.float32),
            pltpu.VMEM(out, jnp.float32),
            dma((4,)), dma((steps,)), dma((steps,)),
        ],
        name="histogram",
        compiler_params=pltpu.CompilerParams(vmem_limit_bytes=67043328),
    )(leaf, live, codes, grad.reshape(blocks, BLOCK), hess.reshape(blocks, BLOCK))


MESH = pl.DeviceIdType.MESH
MIN_CHILD = 20
ridge_term = 1.0


def finish(x):
    flat = x.reshape(192, 128)
    row = lax.broadcasted_iota(jnp.int32, (128, 256), 0)
    col = lax.broadcasted_iota(jnp.int32, (128, 256), 1)
    same = 2 * (row // 64) + row // 8 % 2 == (col % 128) // LO
    upto = 8 * (row // 16 % 4) + row % 8 <= col % LO
    upper = jnp.where(same & (upto | (col >= 128)), 1.0, 0.0)
    sums = jnp.dot(flat, upper, precision=lax.Precision.HIGHEST, preferred_element_type=jnp.float32)
    sub = lax.broadcasted_iota(jnp.int32, (8, 128), 0)
    gains, tops = [], []
    for leaf in range(2):
        top = None
        for q in range(4):
            left, total = [], []
            for s in range(3):
                at = ((leaf * 4 + q) * 3 + s) * 8
                inner, whole = sums[at:at + 8, :128], sums[at:at + 8, 128:]
                run = whole
                for d in (1, 2, 4):
                    run = run + jnp.where(sub >= d, pltpu.roll(run, d, 0), 0.0)
                left.append(inner + (run - whole))
                total.append(jnp.broadcast_to(run[7:8, :], (8, 128)))
            right = [t - v for t, v in zip(total, left)]
            raw = 0.5 * (
                left[0] ** 2 / (left[1] + ridge_term)
                + right[0] ** 2 / (right[1] + ridge_term)
                - total[0] ** 2 / (total[1] + ridge_term)
            )
            allowed = (left[2] >= MIN_CHILD) & (right[2] >= MIN_CHILD)
            gain = jnp.where(allowed, raw, 0.0)
            gains.append(gain)
            top = gain if top is None else jnp.maximum(top, gain)
        tops.append(jnp.broadcast_to(jnp.max(top), (2, 128)))
    return gains, jnp.where(sub[:2] == 0, tops[0], tops[1])


def exchange_kernel(hist, gain_ref, best_ref, own, part, hop1, hop2, peak8, peak16,
                    load_sem, s0, r0, s1, r1, s2, r2, sa, ra, sb, rb):
    r = lax.axis_index("rows")
    x = lax.axis_index("feat")
    c = r % 2
    z = (r // 2) % 4
    y = r // 8
    at = (y, z)

    def rows_id(yy, zz, cc):
        return {"rows": (yy * 4 + zz) * 2 + cc, "feat": x}

    def along(axis, step):
        return rows_id((y + step) % 4, z, c) if axis == 0 else rows_id(y, (z + step) % 4, c)

    def octet(d):
        i = (x * 2 + c + d) % 8
        return {"rows": (y * 4 + z) * 2 + i % 2, "feat": i // 2}

    def plane(d):
        return {"rows": ((y * 4 + z + d) % 16) * 2 + c, "feat": x}

    barrier = pltpu.get_barrier_semaphore()
    for d in range(1, 8):
        pl.semaphore_signal(barrier, inc=1, device_id=octet(d), device_id_type=MESH)
    for axis in range(2):
        for step in (1, 2, 3):
            pl.semaphore_signal(barrier, inc=1, device_id=along(axis, step), device_id_type=MESH)

    order = (2, 1, 3, 0)

    def source(leaf, k, core):
        i = (at[leaf] + order[k]) % 4
        return hist.at[i, :, core, leaf] if leaf == 0 else hist.at[:, i, core, leaf]

    loads = [[pltpu.make_async_copy(source(leaf, k, c), own.at[leaf, k], load_sem.at[leaf, k])
              for k in range(4)] for leaf in range(2)]
    for k in range(4):
        for leaf in range(2):
            loads[leaf][k].start()
    pl.semaphore_wait(barrier, 13)

    pairs = [[pltpu.make_async_remote_copy(
        src_ref=source(leaf, k, 1 - c), dst_ref=part.at[leaf, k],
        send_sem=s0.at[leaf, k], recv_sem=r0.at[leaf, k],
        device_id=rows_id(y, z, 1 - c), device_id_type=MESH)
        for k in range(4)] for leaf in range(2)]
    for k in range(4):
        for leaf in range(2):
            pairs[leaf][k].start()

    def send1(leaf, way, i, k, b):
        return pltpu.make_async_remote_copy(
            src_ref=own.at[leaf, k, pl.ds(b, 2)], dst_ref=hop1.at[leaf, way, i],
            send_sem=s1.at[leaf, way, i], recv_sem=r1.at[leaf, way, i],
            device_id=along(leaf, 1 if way == 0 else 3), device_id_type=MESH)

    first = [[[send1(leaf, 0, 0, 0, 0), send1(leaf, 0, 1, 1, 2), send1(leaf, 0, 2, 1, 0)],
              [send1(leaf, 1, 0, 0, 2), send1(leaf, 1, 1, 2, 0), send1(leaf, 1, 2, 2, 2)]] for leaf in range(2)]

    def ready(leaf, k):
        loads[leaf][k].wait()
        pairs[leaf][k].wait_recv()
        own[leaf, k] = own[leaf, k] + part[leaf, k]

    for leaf in range(2):
        ready(leaf, 0)
        first[leaf][0][0].start()
        first[leaf][1][0].start()
    for leaf in range(2):
        ready(leaf, 1)
        first[leaf][0][1].start()
        ready(leaf, 2)
        first[leaf][1][1].start()
    for leaf in range(2):
        first[leaf][0][0].wait_recv()
        own[leaf, 1, 0:2] = own[leaf, 1, 0:2] + hop1[leaf, 0, 0]
        first[leaf][0][2].start()
        first[leaf][1][0].wait_recv()
        own[leaf, 2, 2:4] = own[leaf, 2, 2:4] + hop1[leaf, 1, 0]
        first[leaf][1][2].start()
    for leaf in range(2):
        ready(leaf, 3)

    def send2(leaf, step):
        return pltpu.make_async_remote_copy(
            src_ref=own.at[leaf, 3, (at[1 - leaf] + step) % 4], dst_ref=hop2.at[leaf, step - 1],
            send_sem=s2.at[leaf, step - 1], recv_sem=r2.at[leaf, step - 1],
            device_id=along(1 - leaf, step), device_id_type=MESH)

    second = [[send2(leaf, step) for step in (2, 1, 3)] for leaf in range(2)]
    for leaf in range(2):
        for way, i in ((0, 1), (1, 1), (0, 2), (1, 2)):
            first[leaf][way][i].wait_recv()
        own[leaf, 3, 0:2] = own[leaf, 3, 0:2] + (hop1[leaf, 0, 2] + hop1[leaf, 1, 1])
        own[leaf, 3, 2:4] = own[leaf, 3, 2:4] + (hop1[leaf, 0, 1] + hop1[leaf, 1, 2])
        for copy in second[leaf]:
            copy.start()
    mine = []
    for leaf in range(2):
        for copy in second[leaf]:
            copy.wait_recv()
        mine.append((own[leaf, 3, at[1 - leaf]] + hop2[leaf, 0]) + (hop2[leaf, 1] + hop2[leaf, 2]))

    gains, top = finish(jnp.concatenate(mine, 0))
    for i, gain in enumerate(gains):
        gain_ref[i // 4, i % 4] = gain

    def spread(peaks, n, ssem, rsem, to):
        copies = [pltpu.make_async_remote_copy(
            src_ref=peaks.at[0], dst_ref=peaks.at[d], send_sem=ssem.at[d], recv_sem=rsem.at[d],
            device_id=to(d), device_id_type=MESH) for d in range(1, n)]
        for copy in copies:
            copy.start()
        for copy in copies:
            copy.wait()

    peak16[0] = top
    spread(peak16, 16, sb, rb, plane)
    peak8[0] = jnp.max(peak16[...], 0)
    spread(peak8, 8, sa, ra, octet)
    best_ref[...] = jnp.max(peak8[...], 0)

    for leaf in range(2):
        for k in range(4):
            pairs[leaf][k].wait_send()
        for way in range(2):
            for i in range(3):
                first[leaf][way][i].wait_send()
        for copy in second[leaf]:
            copy.wait_send()


def exchange(hist):
    dma = pltpu.SemaphoreType.DMA
    return pl.pallas_call(
        exchange_kernel,
        out_shape=(
            jax.ShapeDtypeStruct((2, 4, HI, 128), jnp.float32),
            jax.ShapeDtypeStruct((2, 128), jnp.float32),
        ),
        in_specs=[pl.BlockSpec(memory_space=pl.ANY)],
        out_specs=(pl.BlockSpec(memory_space=pltpu.VMEM), pl.BlockSpec(memory_space=pltpu.VMEM)),
        scratch_shapes=[
            pltpu.VMEM((2, 4, 4, 96, 128), jnp.float32),
            pltpu.VMEM((2, 4, 4, 96, 128), jnp.float32),
            pltpu.VMEM((2, 2, 3, 2, 96, 128), jnp.float32),
            pltpu.VMEM((2, 3, 96, 128), jnp.float32),
            pltpu.VMEM((8, 2, 128), jnp.float32),
            pltpu.VMEM((16, 2, 128), jnp.float32),
            dma((2, 4)), dma((2, 4)), dma((2, 4)),
            dma((2, 2, 3)), dma((2, 2, 3)), dma((2, 3)), dma((2, 3)),
            dma((8,)), dma((8,)), dma((16,)), dma((16,)),
        ],
        name="exchange",
        compiler_params=pltpu.CompilerParams(collective_id=0, has_side_effects=True, vmem_limit_bytes=54525952),
    )(hist.reshape(4, 4, 2, 2, 96, 128))


def local(bin_codes, gradient, hessian, leaf_of_block, block_rows):
    mine = local_hist(bin_codes, gradient, hessian, leaf_of_block, block_rows)
    gain, best = exchange(mine)
    split_gain = gain.reshape(2, 4, HI, 4, LO).transpose(0, 1, 3, 2, 4).reshape(2, 16, BINS)
    return split_gain, best[:, 0]


def solution(mesh):
    return jax.shard_map(
        local,
        mesh=mesh,
        in_specs=(P("rows", "feat"), P("rows"), P("rows"), P("rows"), P("rows")),
        out_specs=(P(None, ("feat", "rows"), None), P()),
        check_vma=False,
    )
```

```python
import jax
import jax.numpy as jnp
from jax import lax
from jax.experimental import pallas as pl
from jax.experimental.pallas import tpu as pltpu
from jax._src.pallas.mosaic.core import AccMemorySpace
from jax.sharding import PartitionSpec as P

BINS = 256
BLOCK = 128
LO = 32
HI = 8
FSTEP = 128
GROUP = 8
GROUPS = 8
TILE = 256


def hist_kernel(leaf_hbm, live_hbm, codes_hbm, grad_hbm, hess_hbm, out_hbm,
                leaf_ref, live_ref, table, codes_ref, grad_ref, hess_ref, lo_ref, hi_ref,
                g_ref, h_ref, c_ref, stat_ref, gf, hf, out_ref, small_sem, code_sem, out_sem):
    blocks = leaf_ref.shape[0]
    steps = codes_ref.shape[0]
    per_table = table.shape[0] // 2
    bf16 = jnp.bfloat16

    small = [pltpu.make_async_copy(a, b, small_sem.at[i]) for i, (a, b) in enumerate(
        ((leaf_hbm, leaf_ref), (live_hbm, live_ref), (grad_hbm, grad_ref), (hess_hbm, hess_ref)))]
    for copy in small:
        copy.start()

    def codes_copy(i):
        return pltpu.make_async_copy(
            codes_hbm.at[:, pl.ds(pl.multiple_of(i * FSTEP, FSTEP), FSTEP)], codes_ref.at[i], code_sem.at[i])

    codes_copy(0).start()
    stat_ref[...] = jnp.zeros_like(stat_ref)
    for copy in small:
        copy.wait()
    gf[...] = grad_ref[...].astype(jnp.float32)
    hf[...] = hess_ref[...].astype(jnp.float32)
    lane = lax.broadcasted_iota(jnp.int32, (8, 128), 1)
    sub = lax.broadcasted_iota(jnp.int32, (8, 128), 0)

    def place(k4, c):
        off0, off1 = c
        for d in range(4):
            k = k4 * 4 + d
            n = live_ref[k]
            leaf = leaf_ref[k]
            off = jnp.where(leaf == 0, off0, off1)
            to = leaf * per_table + off
            shift = k * BLOCK - 8 * off
            for i in range(BLOCK // 8):
                table[to + i] = shift
            g = jnp.broadcast_to(gf[pl.ds(k, 1), :], (8, 128))
            h = jnp.broadcast_to(hf[pl.ds(k, 1), :], (8, 128))
            s = jnp.where(sub == 0, g, jnp.where(sub == 1, h, jnp.where(sub == 2, 1.0, 0.0)))
            s = jnp.where(lane < n, s, 0.0)
            turned = lax.rem(off, 16) * 8
            rolled = pltpu.roll(s, turned, 1)
            at = off // 16
            stat_ref[leaf, at] += jnp.where(lane >= turned, rolled, 0.0)
            stat_ref[leaf, at + 1] += jnp.where(lane < turned, rolled, 0.0)
            off = off + (n + 7) // 8
            off0 = jnp.where(leaf == 0, off, off0)
            off1 = jnp.where(leaf == 0, off1, off)
        return off0, off1

    ends = lax.fori_loop(0, blocks // 4, place, (jnp.int32(0), jnp.int32(0)))
    tiles = [(end * 8 + TILE - 1) // TILE for end in ends]
    for leaf in range(2):
        for i in range(TILE // 8):
            table[leaf * per_table + ends[leaf] + i] = -8 * ends[leaf]

        @pl.loop(0, tiles[leaf])
        def _(t):
            for half in range(2):
                s = stat_ref[leaf, 2 * t + half]
                for i, ref in enumerate((g_ref, h_ref, c_ref)):
                    ref[leaf, t, :, half * 128:half * 128 + 128] = jnp.broadcast_to(s[i:i + 1, :], (16, 128)).astype(bf16)

    sub8 = lax.broadcasted_iota(jnp.int32, (16, TILE), 0) % 8
    lo_n = [(sub8 + 8 * k).astype(jnp.float32).astype(bf16) for k in range(4)]
    hi_n = lo_n[0]
    one = jnp.ones((16, TILE), bf16)
    zero = jnp.zeros((16, TILE), bf16)
    which = 2 * (lane // 64) + lane // 8 % 2

    def turn(step, leaf, t, half):
        first = t * (TILE // 8) + half * (BLOCK // 8)
        rows = [codes_ref[step, pl.ds(pl.multiple_of(table[leaf * per_table + first + i] + 8 * (first + i), 8), 8), :]
                for i in range(BLOCK // 8)]
        word = jnp.concatenate(rows, 0).T
        lanes = slice(BLOCK * half, BLOCK * half + BLOCK)
        to = (0 if leaf == 0 else tiles[0]) + t
        lo_ref[step % 2, to, :, lanes] = (word & (LO - 1)).astype(jnp.float32)
        hi_ref[step % 2, to, :, lanes] = (word >> 5).astype(jnp.float32)

    codes_copy(0).wait()
    for i in range(1, steps):
        codes_copy(i).start()
    for leaf in range(2):
        @pl.loop(0, tiles[leaf])
        def _(t):
            for half in range(2):
                turn(0, leaf, t, half)

    @pl.loop(0, steps)
    def _(step):
        slot = step % 2
        later = jnp.minimum(step + 1, steps - 1)

        @pl.when(step + 1 < steps)
        def _():
            codes_copy(later).wait()

        for leaf in range(2):
            base = 0 if leaf == 0 else tiles[0]
            for half in range(FSTEP // (GROUPS * GROUP)):
                def run(*accs, leaf=leaf, half=half, base=base):
                    def pair(ref, t, i, p):
                        f = (half * GROUPS + i) * GROUP + 2 * p
                        return jnp.concatenate([jnp.broadcast_to(ref[slot, base + t, f + d:f + d + 1, :], (8, TILE))
                                                for d in range(2)], 0).astype(bf16)

                    def push(t, i):
                        rhs = []
                        for p in range(GROUP // 2):
                            low = pair(lo_ref, t, i, p)
                            rhs += [jnp.where(low == n, one, zero) for n in lo_n]
                        hot = jnp.concatenate(rhs, 0).astype(jnp.float8_e4m3fn)
                        pltpu.matmul_push_rhs(hot, (i // 2) % 2, i % 2, transpose=True)

                    def tile_step(t, carry):
                        stats = [ref[leaf, t] for ref in (g_ref, h_ref, c_ref)]
                        for i in range(GROUPS):
                            if i >= 2:
                                push(t, i)
                            lhs = []
                            for p in range(GROUP // 2):
                                hit = pair(hi_ref, t, i, p) == hi_n
                                lhs += [jnp.where(hit, s, zero) for s in stats]
                            pltpu.matmul_acc_lhs(accs[i], jnp.concatenate(lhs, 0), load_staged_rhs=(i // 2) % 2)
                        for i in range(2):
                            push(t + 1, i)
                        turn(later, leaf, t, half)
                        return carry

                    for i in range(2):
                        push(0, i)
                    lax.fori_loop(0, tiles[leaf], tile_step, 0)
                    for i in range(2):
                        pltpu.matmul_acc_lhs(accs[GROUPS + i], zero, load_staged_rhs=0)
                    for i in range(GROUPS):
                        sums = pltpu.matmul_pop(accs[i])
                        for q in range(2):
                            for s in range(3):
                                tile = None
                                for d in range(4):
                                    row = 48 * (2 * q + d // 2) + 16 * s + 8 * (d % 2)
                                    piece = sums[row:row + 8, 128 * q:128 * q + 128]
                                    tile = piece if tile is None else jnp.where(which == d, piece, tile)
                                gq = (half * GROUPS + i) * 2 + q
                                out_ref[step * (FSTEP // 16) + gq // 4, leaf, gq % 4, s] = tile

                pl.run_scoped(run, *[AccMemorySpace(i % 2)((24 * GROUP, 256), jnp.float32) for i in range(GROUPS)],
                              *[AccMemorySpace(i)((16, 256), jnp.float32) for i in range(2)])
        out_copy(out_ref, out_hbm, out_sem, step).start()

    for i in range(steps):
        out_copy(out_ref, out_hbm, out_sem, i).wait()


def out_copy(out_ref, out_hbm, out_sem, i):
    part = pl.ds(i * (FSTEP // 16), FSTEP // 16)
    return pltpu.make_async_copy(out_ref.at[part], out_hbm.at[part], out_sem.at[i])


def local_hist(codes, grad, hess, leaf, live):
    rows, feats = codes.shape
    blocks = leaf.shape[0]
    tiles = rows // TILE
    steps = feats // FSTEP
    hbm = pl.BlockSpec(memory_space=pltpu.HBM)
    out = (feats // 16, 2, 4, 3, 8, 128)
    dma = pltpu.SemaphoreType.DMA
    return pl.pallas_call(
        hist_kernel,
        out_shape=jax.ShapeDtypeStruct(out, jnp.float32),
        in_specs=[hbm] * 5,
        out_specs=hbm,
        scratch_shapes=[
            pltpu.SMEM((blocks,), jnp.int32),
            pltpu.SMEM((blocks,), jnp.int32),
            pltpu.SMEM((2 * (rows // 8 + TILE // 8 + 16),), jnp.int32),
            pltpu.VMEM((steps, rows, FSTEP), jnp.int32),
            pltpu.VMEM((blocks, BLOCK), jnp.bfloat16),
            pltpu.VMEM((blocks, BLOCK), jnp.bfloat16),
            pltpu.VMEM((2, tiles + 2, FSTEP, TILE), jnp.float32),
            pltpu.VMEM((2, tiles + 2, FSTEP, TILE), jnp.float32),
            pltpu.VMEM((2, tiles, 16, TILE), jnp.bfloat16),
            pltpu.VMEM((2, tiles, 16, TILE), jnp.bfloat16),
            pltpu.VMEM((2, tiles, 16, TILE), jnp.bfloat16),
            pltpu.VMEM((2, 2 * tiles + 2, 8, 128), jnp.float32),
            pltpu.VMEM((blocks, BLOCK), jnp.float32),
            pltpu.VMEM((blocks, BLOCK), jnp.float32),
            pltpu.VMEM(out, jnp.float32),
            dma((4,)), dma((steps,)), dma((steps,)),
        ],
        name="histogram",
        compiler_params=pltpu.CompilerParams(vmem_limit_bytes=67043328),
    )(leaf, live, codes, grad.reshape(blocks, BLOCK), hess.reshape(blocks, BLOCK))


MESH = pl.DeviceIdType.MESH
MIN_CHILD = 20
ridge_term = 1.0


def finish(x):
    flat = x.reshape(192, 128)
    row = lax.broadcasted_iota(jnp.int32, (128, 256), 0)
    col = lax.broadcasted_iota(jnp.int32, (128, 256), 1)
    same = 2 * (row // 64) + row // 8 % 2 == (col % 128) // LO
    upto = 8 * (row // 16 % 4) + row % 8 <= col % LO
    upper = jnp.where(same & (upto | (col >= 128)), 1.0, 0.0)
    sums = jnp.dot(flat, upper, precision=lax.Precision.HIGHEST, preferred_element_type=jnp.float32)
    sub = lax.broadcasted_iota(jnp.int32, (8, 128), 0)
    gains, tops = [], []
    for leaf in range(2):
        top = None
        for q in range(4):
            left, total = [], []
            for s in range(3):
                at = ((leaf * 4 + q) * 3 + s) * 8
                inner, whole = sums[at:at + 8, :128], sums[at:at + 8, 128:]
                run = whole
                for d in (1, 2, 4):
                    run = run + jnp.where(sub >= d, pltpu.roll(run, d, 0), 0.0)
                left.append(inner + (run - whole))
                total.append(jnp.broadcast_to(run[7:8, :], (8, 128)))
            right = [t - v for t, v in zip(total, left)]
            raw = 0.5 * (
                left[0] ** 2 / (left[1] + ridge_term)
                + right[0] ** 2 / (right[1] + ridge_term)
                - total[0] ** 2 / (total[1] + ridge_term)
            )
            allowed = (left[2] >= MIN_CHILD) & (right[2] >= MIN_CHILD)
            gain = jnp.where(allowed, raw, 0.0)
            gains.append(gain)
            top = gain if top is None else jnp.maximum(top, gain)
        tops.append(jnp.broadcast_to(jnp.max(top), (2, 128)))
    return gains, jnp.where(sub[:2] == 0, tops[0], tops[1])


def exchange_kernel(hist, gain_ref, best_ref, own, part, hop1, hop2, peak8, peak16,
                    load_sem, s0, r0, s1, r1, s2, r2, sa, ra, sb, rb):
    r = lax.axis_index("rows")
    x = lax.axis_index("feat")
    c = r % 2
    z = (r // 2) % 4
    y = r // 8
    at = (y, z)

    def rows_id(yy, zz, cc):
        return {"rows": (yy * 4 + zz) * 2 + cc, "feat": x}

    def along(axis, step):
        return rows_id((y + step) % 4, z, c) if axis == 0 else rows_id(y, (z + step) % 4, c)

    def octet(d):
        i = (x * 2 + c + d) % 8
        return {"rows": (y * 4 + z) * 2 + i % 2, "feat": i // 2}

    def plane(d):
        return {"rows": ((y * 4 + z + d) % 16) * 2 + c, "feat": x}

    barrier = pltpu.get_barrier_semaphore()
    for d in range(1, 8):
        pl.semaphore_signal(barrier, inc=1, device_id=octet(d), device_id_type=MESH)
    for axis in range(2):
        for step in (1, 2, 3):
            pl.semaphore_signal(barrier, inc=1, device_id=along(axis, step), device_id_type=MESH)

    order = (2, 1, 3, 0)

    def source(leaf, k, core):
        i = (at[leaf] + order[k]) % 4
        return hist.at[i, :, core, leaf] if leaf == 0 else hist.at[:, i, core, leaf]

    loads = [[pltpu.make_async_copy(source(leaf, k, c), own.at[leaf, k], load_sem.at[leaf, k])
              for k in range(4)] for leaf in range(2)]
    for k in range(4):
        for leaf in range(2):
            loads[leaf][k].start()
    pl.semaphore_wait(barrier, 13)

    pairs = [[pltpu.make_async_remote_copy(
        src_ref=source(leaf, k, 1 - c), dst_ref=part.at[leaf, k],
        send_sem=s0.at[leaf, k], recv_sem=r0.at[leaf, k],
        device_id=rows_id(y, z, 1 - c), device_id_type=MESH)
        for k in range(4)] for leaf in range(2)]
    for k in range(4):
        for leaf in range(2):
            pairs[leaf][k].start()

    def send1(leaf, way, i, k, b):
        return pltpu.make_async_remote_copy(
            src_ref=own.at[leaf, k, pl.ds(b, 2)], dst_ref=hop1.at[leaf, way, i],
            send_sem=s1.at[leaf, way, i], recv_sem=r1.at[leaf, way, i],
            device_id=along(leaf, 1 if way == 0 else 3), device_id_type=MESH)

    first = [[[send1(leaf, 0, 0, 0, 0), send1(leaf, 0, 1, 1, 2), send1(leaf, 0, 2, 1, 0)],
              [send1(leaf, 1, 0, 0, 2), send1(leaf, 1, 1, 2, 0), send1(leaf, 1, 2, 2, 2)]] for leaf in range(2)]

    def ready(leaf, k):
        loads[leaf][k].wait()
        pairs[leaf][k].wait_recv()
        own[leaf, k] = own[leaf, k] + part[leaf, k]

    for leaf in range(2):
        ready(leaf, 0)
        first[leaf][0][0].start()
        first[leaf][1][0].start()
    for leaf in range(2):
        ready(leaf, 1)
        first[leaf][0][0].wait_send()
        first[leaf][0][1].start()
        ready(leaf, 2)
        first[leaf][1][0].wait_send()
        first[leaf][1][1].start()
    for leaf in range(2):
        first[leaf][0][0].wait_recv()
        own[leaf, 1, 0:2] = own[leaf, 1, 0:2] + hop1[leaf, 0, 0]
        first[leaf][0][2].start()
        first[leaf][1][0].wait_recv()
        own[leaf, 2, 2:4] = own[leaf, 2, 2:4] + hop1[leaf, 1, 0]
        first[leaf][1][2].start()
    for leaf in range(2):
        ready(leaf, 3)

    def send2(leaf, step):
        return pltpu.make_async_remote_copy(
            src_ref=own.at[leaf, 3, (at[1 - leaf] + step) % 4], dst_ref=hop2.at[leaf, step - 1],
            send_sem=s2.at[leaf, step - 1], recv_sem=r2.at[leaf, step - 1],
            device_id=along(1 - leaf, step), device_id_type=MESH)

    second = [[send2(leaf, step) for step in (2, 1, 3)] for leaf in range(2)]
    for leaf in range(2):
        for way, i in ((0, 1), (1, 1), (0, 2), (1, 2)):
            first[leaf][way][i].wait_recv()
        own[leaf, 3, 0:2] = own[leaf, 3, 0:2] + (hop1[leaf, 0, 2] + hop1[leaf, 1, 1])
        own[leaf, 3, 2:4] = own[leaf, 3, 2:4] + (hop1[leaf, 0, 1] + hop1[leaf, 1, 2])
        for copy in second[leaf]:
            copy.start()
    mine = []
    for leaf in range(2):
        for copy in second[leaf]:
            copy.wait_recv()
        mine.append((own[leaf, 3, at[1 - leaf]] + hop2[leaf, 0]) + (hop2[leaf, 1] + hop2[leaf, 2]))

    gains, top = finish(jnp.concatenate(mine, 0))
    for i, gain in enumerate(gains):
        gain_ref[i // 4, i % 4] = gain

    def spread(peaks, n, ssem, rsem, to):
        copies = [pltpu.make_async_remote_copy(
            src_ref=peaks.at[0], dst_ref=peaks.at[d], send_sem=ssem.at[d], recv_sem=rsem.at[d],
            device_id=to(d), device_id_type=MESH) for d in range(1, n)]
        for copy in copies:
            copy.start()
        for copy in copies:
            copy.wait_recv()
        return copies

    peak16[0] = top
    sent = spread(peak16, 16, sb, rb, plane)
    peak8[0] = jnp.max(peak16[...], 0)
    sent += spread(peak8, 8, sa, ra, octet)
    best_ref[...] = jnp.max(peak8[...], 0)

    for copy in sent:
        copy.wait_send()
    for leaf in range(2):
        for k in range(4):
            pairs[leaf][k].wait_send()
        for way in range(2):
            for i in range(1, 3):
                first[leaf][way][i].wait_send()
        for copy in second[leaf]:
            copy.wait_send()


def exchange(hist):
    dma = pltpu.SemaphoreType.DMA
    return pl.pallas_call(
        exchange_kernel,
        out_shape=(
            jax.ShapeDtypeStruct((2, 4, HI, 128), jnp.float32),
            jax.ShapeDtypeStruct((2, 128), jnp.float32),
        ),
        in_specs=[pl.BlockSpec(memory_space=pl.ANY)],
        out_specs=(pl.BlockSpec(memory_space=pltpu.VMEM), pl.BlockSpec(memory_space=pltpu.VMEM)),
        scratch_shapes=[
            pltpu.VMEM((2, 4, 4, 96, 128), jnp.float32),
            pltpu.VMEM((2, 4, 4, 96, 128), jnp.float32),
            pltpu.VMEM((2, 2, 3, 2, 96, 128), jnp.float32),
            pltpu.VMEM((2, 3, 96, 128), jnp.float32),
            pltpu.VMEM((8, 2, 128), jnp.float32),
            pltpu.VMEM((16, 2, 128), jnp.float32),
            dma((2, 4)), dma((2, 4)), dma((2, 4)),
            dma((2, 2, 3)), dma((2, 2, 3)), dma((2, 3)), dma((2, 3)),
            dma((8,)), dma((8,)), dma((16,)), dma((16,)),
        ],
        name="exchange",
        compiler_params=pltpu.CompilerParams(collective_id=0, has_side_effects=True, vmem_limit_bytes=54525952),
    )(hist.reshape(4, 4, 2, 2, 96, 128))


def local(bin_codes, gradient, hessian, leaf_of_block, block_rows):
    mine = local_hist(bin_codes, gradient, hessian, leaf_of_block, block_rows)
    gain, best = exchange(mine)
    split_gain = gain.reshape(2, 4, HI, 4, LO).transpose(0, 1, 3, 2, 4).reshape(2, 16, BINS)
    return split_gain, best[:, 0]


def solution(mesh):
    return jax.shard_map(
        local,
        mesh=mesh,
        in_specs=(P("rows", "feat"), P("rows"), P("rows"), P("rows"), P("rows")),
        out_specs=(P(None, ("feat", "rows"), None), P()),
        check_vma=False,
    )
```
